32 devices in a mesh: outer: 4 (over z), inner: 2 (over x), chan: 4 (over y, core).
Axes of the slice: x: 2, y: 2, z: 4, core: 2. Of those that a mesh axis runs over, the one named last changes fastest.
Arguments:
- gate_proj: bfloat16 [128, 65536], P('chan', ('outer', 'inner')), may hold values from -6 to 6
- key_proj: bfloat16 [128, 65536], P('chan', ('outer', 'inner')), may hold values from -6 to 6
- value_proj: bfloat16 [128, 65536], P('chan', ('outer', 'inner')), may hold values from -6 to 6
- filter_taps: float32 [65536], P(('outer', 'inner', 'chan')), may hold values from -1 to 1, as said below
- skip_gain: float32 [128], P('chan'), may hold values from 0.5 to 1.5
Outputs:
- hyena_out: float32 [128, 65536], P('chan', ('outer', 'inner'))
The draws below stay inside these ranges and needn't reach their ends.
Inputs may be any that keep to these rules, and one draw needn't show every extreme that they name: `filter_taps`: one filter for all 128 channels.
All inputs are finite; a program needn't handle non-finite values.
Results may differ from the reference program's by a relative error of at most 0.0003.
Values sent between devices are 32-bit elements; how exact they have to be, the bound alone decides.
A program may use at most 128 MiB of HBM per device.

```python
import jax
import jax.numpy as jnp
from jax import lax

CH = 128
SEQ = 65536


def draw_filter_taps(key, part):
    base = jax.random.fold_in(key, 17)
    key_fast, key_slow, key_noise = jax.random.split(base, 3)
    lags = jnp.arange(SEQ).astype(jnp.float32)
    tau_fast = jax.random.uniform(key_fast, (), jnp.float32, 30.0, 50.0)
    tau_slow = jax.random.uniform(key_slow, (), jnp.float32, 0.5, 1.5) * SEQ
    energy_fast = -jnp.expm1(-2.0 * SEQ / tau_fast) / -jnp.expm1(-2.0 / tau_fast)
    energy_slow = -jnp.expm1(-2.0 * SEQ / tau_slow) / -jnp.expm1(-2.0 / tau_slow)
    power = 0.3 * jnp.exp(-2.0 * lags / tau_fast) / energy_fast + 0.7 * jnp.exp(-2.0 * lags / tau_slow) / energy_slow
    noise = jnp.clip(jax.random.normal(key_noise, (SEQ,), jnp.float32), -5.0, 5.0)
    return (noise * jnp.sqrt(power)).astype(jnp.float32)


def block_levels(rng, shape, pieces, smallest, top_value):
    factor_of, own = 1.0, jax.random.fold_in(rng, 6)
    for position, shards_of in pieces:
        draws = jnp.exp(jax.random.uniform(jax.random.fold_in(own, position), (shards_of,), jnp.float32, smallest / len(pieces), top_value / len(pieces)))
        factor_of = factor_of * jnp.repeat(draws, shape[position] // shards_of).reshape([-1 if axis == position else 1 for axis in range(len(shape))])
    return factor_of


def centred(own_key, extent, deviation, reach, cuts=(), dtype=jnp.bfloat16):
    entries = deviation * jax.random.normal(own_key, extent, jnp.float32)
    if cuts:
        entries = entries * block_levels(own_key, extent, cuts, -0.22, 0.18)
    return jnp.clip(entries, -reach, reach).astype(dtype)


def setup_inputs(seed: int = 0) -> dict:
    splits = jax.random.split(jax.random.key(seed), 6)
    return {
        "gate_proj": centred(splits[0], (CH, SEQ), 1.0, 6.0, ((0, 4), (1, 8))),
        "key_proj": centred(splits[1], (CH, SEQ), 1.0, 6.0, ((0, 4), (1, 8))),
        "value_proj": centred(splits[2], (CH, SEQ), 1.0, 6.0, ((0, 4), (1, 8))),
        "filter_taps": draw_filter_taps(jax.random.fold_in(splits[5], 71), 0),
        "skip_gain": jnp.clip(0.5 + 1.0 * jax.random.uniform(splits[4], (CH,), jnp.float32) ** block_levels(splits[4], (CH,), ((0, 4),), -0.2, 0.2), 0.5, 1.5),
    }


def convolve_block(block_signal, spectrum):
    padded = jnp.fft.rfft(block_signal, n=2 * SEQ, axis=-1)
    return jnp.fft.irfft(padded * spectrum[None, :], n=2 * SEQ, axis=-1)[:, :SEQ]


def reference(gate_proj, key_proj, value_proj, filter_taps, skip_gain):
    signal = key_proj.astype(jnp.float32) * value_proj.astype(jnp.float32)
    spectrum = jnp.fft.rfft(filter_taps, n=2 * SEQ)
    blocks = signal.reshape(CH // 16, 16, SEQ)
    conv = lax.map(lambda block: convolve_block(block, spectrum), blocks).reshape(CH, SEQ)
    conv = conv.astype(jnp.float32)
    return gate_proj.astype(jnp.float32) * (conv + skip_gain[:, None] * signal)
```

```python
import functools
import math

import jax
import jax.numpy as jnp
import numpy as np
from jax import lax
from jax.experimental import pallas as pl
from jax.experimental.pallas import tpu as pltpu
from jax.sharding import PartitionSpec as P

HIGHEST = lax.Precision.HIGHEST


def count_up(length):
    return jnp.arange(length, dtype=jnp.int32)


def unit_table(row_index, col_index, modulus):
    turns = row_index * col_index % modulus
    angles = turns.astype(jnp.float32) * (2.0 * math.pi / modulus)
    return (jnp.cos(angles), jnp.sin(angles))


def multiply(form, left, right):
    return jnp.einsum(form, left, right, precision=HIGHEST)


def turn_forward(real_in, imag_in, cos_tab, sine_tab):
    return (real_in * cos_tab + imag_in * sine_tab, imag_in * cos_tab - real_in * sine_tab)


def turn_backward(real_in, imag_in, cos_tab, sine_tab):
    return (real_in * cos_tab - imag_in * sine_tab, imag_in * cos_tab + real_in * sine_tab)


def column_forward(columns, groups, here, total_len):
    span = columns.shape[2]
    cos_m, sine_m = unit_table(count_up(2 * groups)[:, None], count_up(groups)[None, :], 2 * groups)
    real_col = multiply("am,cmr->car", cos_m, columns)
    imag_col = -multiply("am,cmr->car", sine_m, columns)
    positions = here * span + count_up(span)
    cos_r, sine_r = unit_table(count_up(2 * groups)[:, None], positions[None, :], total_len)
    return turn_forward(real_col, imag_col, cos_r, sine_r)


def column_forward_pair(real_cols, imag_cols, groups, here, total_len):
    span = real_cols.shape[2]
    cos_m, sine_m = unit_table(count_up(2 * groups)[:, None], count_up(groups)[None, :], 2 * groups)
    form = "am,cmr->car"
    real_col = multiply(form, cos_m, real_cols) + multiply(form, sine_m, imag_cols)
    imag_col = multiply(form, cos_m, imag_cols) - multiply(form, sine_m, real_cols)
    positions = here * span + count_up(span)
    cos_r, sine_r = unit_table(count_up(2 * groups)[:, None], positions[None, :], total_len)
    return turn_forward(real_col, imag_col, cos_r, sine_r)


def local_forward(real_in, imag_in):
    lead, pair, block_len = real_in.shape
    inner_len = 128
    outer_len = block_len // inner_len
    real_in = real_in.reshape(lead, pair, outer_len, inner_len)
    imag_in = imag_in.reshape(lead, pair, outer_len, inner_len)
    cos_a, sine_a = unit_table(
        count_up(outer_len)[:, None], count_up(outer_len)[None, :], outer_len
    )
    form_a = "jk,ceks->cejs"
    real_mid = multiply(form_a, cos_a, real_in) + multiply(form_a, sine_a, imag_in)
    imag_mid = multiply(form_a, cos_a, imag_in) - multiply(form_a, sine_a, real_in)
    cos_t, sine_t = unit_table(
        count_up(outer_len)[:, None], count_up(inner_len)[None, :], block_len
    )
    real_mid, imag_mid = turn_forward(real_mid, imag_mid, cos_t, sine_t)
    cos_b, sine_b = unit_table(
        count_up(inner_len)[:, None], count_up(inner_len)[None, :], inner_len
    )
    form_b = "cejs,st->cejt"
    real_out = multiply(form_b, real_mid, cos_b) + multiply(form_b, imag_mid, sine_b)
    imag_out = multiply(form_b, imag_mid, cos_b) - multiply(form_b, real_mid, sine_b)
    return (real_out, imag_out)


def local_backward(real_in, imag_in):
    lead, pair, outer_len, inner_len = real_in.shape
    block_len = outer_len * inner_len
    cos_b, sine_b = unit_table(
        count_up(inner_len)[:, None], count_up(inner_len)[None, :], inner_len
    )
    form_b = "cejt,st->cejs"
    real_mid = multiply(form_b, real_in, cos_b) - multiply(form_b, imag_in, sine_b)
    imag_mid = multiply(form_b, imag_in, cos_b) + multiply(form_b, real_in, sine_b)
    cos_t, sine_t = unit_table(
        count_up(outer_len)[:, None], count_up(inner_len)[None, :], block_len
    )
    real_mid, imag_mid = turn_backward(real_mid, imag_mid, cos_t, sine_t)
    cos_a, sine_a = unit_table(
        count_up(outer_len)[:, None], count_up(outer_len)[None, :], outer_len
    )
    form_a = "jk,cejs->ceks"
    real_out = multiply(form_a, cos_a, real_mid) - multiply(form_a, sine_a, imag_mid)
    imag_out = multiply(form_a, cos_a, imag_mid) + multiply(form_a, sine_a, real_mid)
    return (real_out.reshape(lead, pair, block_len), imag_out.reshape(lead, pair, block_len))


def local_columns(gate_proj, key_proj, value_proj, filter_taps, skip_gain):
    outer_count = lax.axis_size("outer")
    inner_count = lax.axis_size("inner")
    groups = outer_count * inner_count
    here = lax.axis_index(("outer", "inner"))
    chans, tok_local = gate_proj.shape
    half_chans = chans // 2
    span = tok_local // groups
    total_len = 2 * groups * tok_local
    signal = key_proj.astype(jnp.float32) * value_proj.astype(jnp.float32)
    taps_local = lax.all_gather(filter_taps, "chan", axis=0, tiled=True)
    sig_cols, tap_cols = (
        lax.all_to_all(
            signal.reshape(chans, groups, span),
            ("outer", "inner"),
            split_axis=1,
            concat_axis=1,
            tiled=True,
        ),
        lax.all_to_all(
            taps_local.reshape(1, groups, span),
            ("outer", "inner"),
            split_axis=1,
            concat_axis=1,
            tiled=True,
        ),
    )
    sig_real, sig_imag = column_forward_pair(
        sig_cols[:half_chans], sig_cols[half_chans:], groups, here, total_len
    )
    tap_real, tap_imag = column_forward(tap_cols, groups, here, total_len)
    sig_real, sig_imag, tap_real, tap_imag = (
        lax.all_to_all(sig_real, ("outer", "inner"), split_axis=1, concat_axis=2, tiled=True),
        lax.all_to_all(sig_imag, ("outer", "inner"), split_axis=1, concat_axis=2, tiled=True),
        lax.all_to_all(tap_real, ("outer", "inner"), split_axis=1, concat_axis=2, tiled=True),
        lax.all_to_all(tap_imag, ("outer", "inner"), split_axis=1, concat_axis=2, tiled=True),
    )
    sig_real, sig_imag = local_forward(sig_real, sig_imag)
    tap_real, tap_imag = local_forward(tap_real, tap_imag)
    prod_real = sig_real * tap_real - sig_imag * tap_imag
    prod_imag = sig_real * tap_imag + sig_imag * tap_real
    back_real, back_imag = local_backward(prod_real, prod_imag)
    back_real, back_imag = (
        lax.all_to_all(back_real, ("outer", "inner"), split_axis=2, concat_axis=1, tiled=True),
        lax.all_to_all(back_imag, ("outer", "inner"), split_axis=2, concat_axis=1, tiled=True),
    )
    positions = here * span + count_up(span)
    cos_r, sine_r = unit_table(count_up(2 * groups)[:, None], positions[None, :], total_len)
    back_real, back_imag = turn_backward(back_real, back_imag, cos_r, sine_r)
    cos_m, sine_m = unit_table(count_up(2 * groups)[:, None], count_up(groups)[None, :], 2 * groups)
    form_m = "am,car->cmr"
    conv_real = multiply(form_m, cos_m, back_real) - multiply(form_m, sine_m, back_imag)
    conv_imag = multiply(form_m, cos_m, back_imag) + multiply(form_m, sine_m, back_real)
    conv_cols = jnp.concatenate((conv_real, conv_imag), axis=0)
    conv_cols = conv_cols * (1.0 / total_len)
    conv = lax.all_to_all(
        conv_cols, ("outer", "inner"), split_axis=1, concat_axis=2, tiled=True
    ).reshape(chans, tok_local)
    return gate_proj.astype(jnp.float32) * (conv + skip_gain[:, None] * signal)


LANES = 128
COLS = 256
MESH = pl.DeviceIdType.MESH


def split_np(table):
    high = table.astype(jnp.bfloat16)
    low = (table - high.astype(np.float64)).astype(jnp.bfloat16)
    return np.stack((high, low))


@functools.lru_cache(maxsize=None)
def dft_tables(rows):
    freqs = 2 * rows
    total_len = freqs * COLS
    angle_a = np.outer(np.arange(freqs), np.arange(freqs)) % freqs * (2.0 * np.pi / freqs)
    cos_a, sine_a = np.cos(angle_a), np.sin(angle_a)
    angle_b = np.outer(np.arange(COLS), np.arange(COLS)) % COLS * (2.0 * np.pi / COLS)
    cos_b, sine_b = np.cos(angle_b), np.sin(angle_b)
    angle_t = np.outer(np.arange(freqs), np.arange(COLS)) * (2.0 * np.pi / total_len)
    return (
        split_np(np.concatenate((cos_a[:, :rows], sine_a[:, :rows]), axis=1)),
        split_np(np.concatenate((cos_a[:rows], sine_a[:rows]), axis=1)),
        split_np(np.block([[cos_b, -sine_b], [sine_b, cos_b]])),
        np.stack((np.cos(angle_t), np.sin(angle_t))).astype(np.float32),
    )


def split(value):
    high = value.astype(jnp.bfloat16)
    return high, (value - high.astype(jnp.float32)).astype(jnp.bfloat16)


def dot(left, right, dims=((1,), (0,))):
    return lax.dot_general(left, right, (dims, ((), ())), preferred_element_type=jnp.float32)


def dot3(left_hi, left_lo, right_hi, right_lo, dims=((1,), (0,))):
    return (
        dot(left_lo, right_hi, dims) + dot(left_hi, right_lo, dims) + dot(left_hi, right_hi, dims)
    )


def conv_kernel(
    sizes,
    sig_ref,
    tap_ref,
    fwd_hbm,
    inv_hbm,
    col_hbm,
    twid_hbm,
    conv_ref,
    xbuf,
    hbuf,
    ybuf,
    rhs,
    back,
    spec,
    fwd,
    inv,
    col,
    twid,
    sig_send,
    sig_recv,
    out_send,
    out_recv,
    tap_send,
    tap_recv,
    spread_send,
    spread_recv,
    own_sem,
    table_sem,
):
    outer_n, inner_n, chan_n = sizes
    groups = outer_n * inner_n
    mine_n = xbuf.shape[0]
    pairs = mine_n // 2
    rows = xbuf.shape[2]
    piece = rows // groups
    freqs = 2 * rows
    step = 256
    outer = lax.axis_index("outer")
    inner = lax.axis_index("inner")
    chan = lax.axis_index("chan")
    here = outer * inner_n + inner
    far = sorted(range(outer_n), key=lambda dz: -min(dz, outer_n - dz))
    hops = [(dz, dx) for dz in far for dx in reversed(range(inner_n)) if dz or dx]
    peers = []
    for dz, dx in hops:
        to_z = lax.rem(outer + dz, outer_n)
        to_x = lax.rem(inner + dx, inner_n)
        peers.append((to_z * inner_n + to_x, (to_z, to_x, chan)))
    sides = [(outer, inner, lax.rem(chan + dc, chan_n)) for dc in range(1, chan_n)]

    barrier = pltpu.get_barrier_semaphore()
    for _, where in peers:
        pl.semaphore_signal(barrier, inc=1, device_id=where, device_id_type=MESH)
    for where in sides:
        pl.semaphore_signal(barrier, inc=1, device_id=where, device_id_type=MESH)
    pl.semaphore_wait(barrier, len(peers) + len(sides))

    def remote(src, dst, send, recv, where):
        copy = pltpu.make_async_remote_copy(
            src_ref=src,
            dst_ref=dst,
            send_sem=send,
            recv_sem=recv,
            device_id=where,
            device_id_type=MESH,
        )
        copy.start()
        return copy

    tap_copies = [
        remote(tap_ref, hbuf.at[:, here, chan], tap_send.at[j], tap_recv.at[j], where)
        for j, (_, where) in enumerate(peers)
    ]
    own = [pltpu.make_async_copy(tap_ref, hbuf.at[:, here, chan], own_sem.at[2 * pairs])]
    own[0].start()
    sig_copies = []
    for pair in range(pairs):
        sig_copies.append(
            [
                remote(
                    sig_ref.at[pl.ds(dest * mine_n + 2 * pair, 2)],
                    xbuf.at[pl.ds(2 * pair, 2), :, pl.ds(here * piece, piece)],
                    sig_send.at[pair, j],
                    sig_recv.at[pair, j],
                    where,
                )
                for j, (dest, where) in enumerate(peers)
            ]
        )
    for pair in range(pairs):
        keep = pltpu.make_async_copy(
            sig_ref.at[pl.ds(here * mine_n + 2 * pair, 2)],
            xbuf.at[pl.ds(2 * pair, 2), :, pl.ds(here * piece, piece)],
            own_sem.at[pair],
        )
        keep.start()
        own.append(keep)
    tables = [
        pltpu.make_async_copy(src, dst, table_sem.at[i])
        for i, (src, dst) in enumerate(
            ((fwd_hbm, fwd), (col_hbm, col), (twid_hbm, twid), (inv_hbm, inv))
        )
    ]
    for copy in tables:
        copy.start()

    own[0].wait()
    for copy in tap_copies:
        copy.wait_recv()
    spread_copies = [
        remote(hbuf.at[:, :, chan], hbuf.at[:, :, chan], spread_send.at[j], spread_recv.at[j], where)
        for j, where in enumerate(sides)
    ]
    for copy in tables:
        copy.wait()
    for copy in spread_copies:
        copy.wait_recv()

    def fill(real, imag):
        for half in range(2):
            for part, at, sign in (
                (real, (0, 0), 1.0),
                (imag, (0, 1), 1.0),
                (imag, (1, 0), 1.0),
                (real, (1, 1), -1.0),
            ):
                lanes = pl.ds(at[1] * COLS + half * LANES, LANES)
                if part is None:
                    high = low = jnp.zeros((rows, LANES), jnp.bfloat16)
                else:
                    high, low = split(sign * part(half))
                rhs[0, pl.ds(at[0] * rows, rows), lanes] = high
                rhs[1, pl.ds(at[0] * rows, rows), lanes] = low

    def forward(at):
        mid = dot3(fwd[0, at, :], fwd[1, at, :], rhs[0], rhs[1])
        real, imag = mid[:, :COLS], mid[:, COLS:]
        cos_t, sine_t = twid[0, at, :], twid[1, at, :]
        turned = jnp.concatenate(turn_forward(real, imag, cos_t, sine_t), axis=1)
        return dot3(*split(turned), col[0], col[1])

    fill(lambda half: hbuf[half].reshape(rows, LANES), None)

    def filter_step(t, carry):
        at = pl.ds(pl.multiple_of(t * step, step), step)
        spec[at, :] = forward(at) * (1.0 / (freqs * COLS))
        return carry

    lax.fori_loop(0, freqs // step, filter_step, 0)

    out_copies = []
    for pair in range(pairs):
        own[1 + pair].wait()
        for copy in sig_copies[pair]:
            copy.wait_recv()
        fill(lambda half: xbuf[2 * pair, half], lambda half: xbuf[2 * pair + 1, half])

        def pair_step(t, carry):
            at = pl.ds(pl.multiple_of(t * step, step), step)
            below = pl.ds(pl.multiple_of(t * step + freqs, step), step)
            freq = forward(at)
            real, imag = freq[:, :COLS], freq[:, COLS:]
            spec_real, spec_imag = spec[at, :COLS], spec[at, COLS:]
            prod = jnp.concatenate(
                (real * spec_real - imag * spec_imag, real * spec_imag + imag * spec_real), axis=1
            )
            mid = dot3(*split(prod), col[0], col[1], ((1,), (1,)))
            cos_t, sine_t = twid[0, at, :], twid[1, at, :]
            real, imag = turn_backward(mid[:, :COLS], mid[:, COLS:], cos_t, sine_t)
            real_hi, real_lo = split(real)
            imag_hi, imag_lo = split(imag)
            back[0, at, :COLS] = real_hi
            back[1, at, :COLS] = real_lo
            back[0, at, COLS:] = imag_hi
            back[1, at, COLS:] = imag_lo
            back[0, below, :COLS] = -imag_hi
            back[1, below, :COLS] = -imag_lo
            back[0, below, COLS:] = real_hi
            back[1, below, COLS:] = real_lo
            return carry

        lax.fori_loop(0, freqs // step, pair_step, 0)
        result = dot3(inv[0], inv[1], back[0], back[1])
        for which in range(2):
            for half in range(2):
                first = which * COLS + half * LANES
                ybuf[2 * pair + which, half] = result[:, first : first + LANES]
        out_copies.append(
            [
                remote(
                    ybuf.at[pl.ds(2 * pair, 2), :, pl.ds(dest * piece, piece)],
                    conv_ref.at[pl.ds(here * mine_n + 2 * pair, 2)],
                    out_send.at[pair, j],
                    out_recv.at[pair, j],
                    where,
                )
                for j, (dest, where) in enumerate(peers)
            ]
        )
        keep = pltpu.make_async_copy(
            ybuf.at[pl.ds(2 * pair, 2), :, pl.ds(here * piece, piece)],
            conv_ref.at[pl.ds(here * mine_n + 2 * pair, 2)],
            own_sem.at[pairs + pair],
        )
        keep.start()
        own.append(keep)

    for pair in range(pairs):
        own[1 + pairs + pair].wait()
        for copy in out_copies[pair]:
            copy.wait_recv()
    for copy in tap_copies + spread_copies + sum(sig_copies, []) + sum(out_copies, []):
        copy.wait_send()


def local_whole(gate_proj, key_proj, value_proj, filter_taps, skip_gain):
    sizes = tuple(lax.axis_size(name) for name in ("outer", "inner", "chan"))
    groups = sizes[0] * sizes[1]
    chans, tok_local = gate_proj.shape
    mine_n = chans // groups
    pairs = mine_n // 2
    piece = tok_local // COLS
    rows = groups * piece
    tap_rows = filter_taps.shape[0] // COLS
    signal = key_proj.astype(jnp.float32) * value_proj.astype(jnp.float32)
    sig_in = signal.reshape(chans, piece, 2, LANES).transpose(0, 2, 1, 3)
    tap_in = filter_taps.reshape(tap_rows, 2, LANES).transpose(1, 0, 2)
    dma = pltpu.SemaphoreType.DMA
    vmem = pl.BlockSpec(memory_space=pltpu.VMEM)
    hbm = pl.BlockSpec(memory_space=pl.ANY)
    tables = dft_tables(rows)
    conv = pl.pallas_call(
        functools.partial(conv_kernel, sizes),
        out_shape=jax.ShapeDtypeStruct((chans, 2, piece, LANES), jnp.float32),
        in_specs=[vmem, vmem, hbm, hbm, hbm, hbm],
        out_specs=vmem,
        scratch_shapes=[
            pltpu.VMEM((mine_n, 2, rows, LANES), jnp.float32),
            pltpu.VMEM((2, groups, sizes[2], tap_rows, LANES), jnp.float32),
            pltpu.VMEM((mine_n, 2, rows, LANES), jnp.float32),
            pltpu.VMEM((2, 2 * rows, 2 * COLS), jnp.bfloat16),
            pltpu.VMEM((2, 4 * rows, 2 * COLS), jnp.bfloat16),
            pltpu.VMEM((2 * rows, 2 * COLS), jnp.float32),
            pltpu.VMEM(tables[0].shape, jnp.bfloat16),
            pltpu.VMEM(tables[1].shape, jnp.bfloat16),
            pltpu.VMEM(tables[2].shape, jnp.bfloat16),
            pltpu.VMEM(tables[3].shape, jnp.float32),
            dma((pairs, groups - 1)),
            dma((pairs, groups - 1)),
            dma((pairs, groups - 1)),
            dma((pairs, groups - 1)),
            dma((groups - 1,)),
            dma((groups - 1,)),
            dma((sizes[2] - 1,)),
            dma((sizes[2] - 1,)),
            dma((2 * pairs + 1,)),
            dma((4,)),
        ],
        compiler_params=pltpu.CompilerParams(
            collective_id=0, has_side_effects=True, vmem_limit_bytes=48 * 1024 * 1024
        ),
    )(sig_in, tap_in, *(jnp.asarray(table) for table in tables))
    conv = conv.transpose(0, 2, 1, 3).reshape(chans, tok_local)
    return gate_proj.astype(jnp.float32) * (conv + skip_gain[:, None] * signal)


def local(gate_proj, key_proj, value_proj, filter_taps, skip_gain):
    groups = lax.axis_size("outer") * lax.axis_size("inner")
    whole_pairs = gate_proj.shape[0] % (2 * groups) == 0
    tiled = gate_proj.shape[1] % (8 * COLS) == 0 and filter_taps.shape[0] % (8 * COLS) == 0
    one = local_whole if whole_pairs and tiled else local_columns
    return one(gate_proj, key_proj, value_proj, filter_taps, skip_gain)


def solution(mesh):
    placed = (
        P("chan", ("outer", "inner")),
        P("chan", ("outer", "inner")),
        P("chan", ("outer", "inner")),
        P(("outer", "inner", "chan")),
        P("chan"),
    )
    return jax.shard_map(
        local, mesh=mesh, in_specs=placed, out_specs=P("chan", ("outer", "inner")), check_vma=False
    )
```

```python
import functools
import math

import jax
import jax.numpy as jnp
import numpy as np
from jax import lax
from jax.experimental import pallas as pl
from jax.experimental.pallas import tpu as pltpu
from jax.sharding import PartitionSpec as P

HIGHEST = lax.Precision.HIGHEST


def count_up(length):
    return jnp.arange(length, dtype=jnp.int32)


def unit_table(row_index, col_index, modulus):
    turns = row_index * col_index % modulus
    angles = turns.astype(jnp.float32) * (2.0 * math.pi / modulus)
    return (jnp.cos(angles), jnp.sin(angles))


def multiply(form, left, right):
    return jnp.einsum(form, left, right, precision=HIGHEST)


def turn_forward(real_in, imag_in, cos_tab, sine_tab):
    return (real_in * cos_tab + imag_in * sine_tab, imag_in * cos_tab - real_in * sine_tab)


def turn_backward(real_in, imag_in, cos_tab, sine_tab):
    return (real_in * cos_tab - imag_in * sine_tab, imag_in * cos_tab + real_in * sine_tab)


def column_forward(columns, groups, here, total_len):
    span = columns.shape[2]
    cos_m, sine_m = unit_table(count_up(2 * groups)[:, None], count_up(groups)[None, :], 2 * groups)
    real_col = multiply("am,cmr->car", cos_m, columns)
    imag_col = -multiply("am,cmr->car", sine_m, columns)
    positions = here * span + count_up(span)
    cos_r, sine_r = unit_table(count_up(2 * groups)[:, None], positions[None, :], total_len)
    return turn_forward(real_col, imag_col, cos_r, sine_r)


def column_forward_pair(real_cols, imag_cols, groups, here, total_len):
    span = real_cols.shape[2]
    cos_m, sine_m = unit_table(count_up(2 * groups)[:, None], count_up(groups)[None, :], 2 * groups)
    form = "am,cmr->car"
    real_col = multiply(form, cos_m, real_cols) + multiply(form, sine_m, imag_cols)
    imag_col = multiply(form, cos_m, imag_cols) - multiply(form, sine_m, real_cols)
    positions = here * span + count_up(span)
    cos_r, sine_r = unit_table(count_up(2 * groups)[:, None], positions[None, :], total_len)
    return turn_forward(real_col, imag_col, cos_r, sine_r)


def local_forward(real_in, imag_in):
    lead, pair, block_len = real_in.shape
    inner_len = 128
    outer_len = block_len // inner_len
    real_in = real_in.reshape(lead, pair, outer_len, inner_len)
    imag_in = imag_in.reshape(lead, pair, outer_len, inner_len)
    cos_a, sine_a = unit_table(
        count_up(outer_len)[:, None], count_up(outer_len)[None, :], outer_len
    )
    form_a = "jk,ceks->cejs"
    real_mid = multiply(form_a, cos_a, real_in) + multiply(form_a, sine_a, imag_in)
    imag_mid = multiply(form_a, cos_a, imag_in) - multiply(form_a, sine_a, real_in)
    cos_t, sine_t = unit_table(
        count_up(outer_len)[:, None], count_up(inner_len)[None, :], block_len
    )
    real_mid, imag_mid = turn_forward(real_mid, imag_mid, cos_t, sine_t)
    cos_b, sine_b = unit_table(
        count_up(inner_len)[:, None], count_up(inner_len)[None, :], inner_len
    )
    form_b = "cejs,st->cejt"
    real_out = multiply(form_b, real_mid, cos_b) + multiply(form_b, imag_mid, sine_b)
    imag_out = multiply(form_b, imag_mid, cos_b) - multiply(form_b, real_mid, sine_b)
    return (real_out, imag_out)


def local_backward(real_in, imag_in):
    lead, pair, outer_len, inner_len = real_in.shape
    block_len = outer_len * inner_len
    cos_b, sine_b = unit_table(
        count_up(inner_len)[:, None], count_up(inner_len)[None, :], inner_len
    )
    form_b = "cejt,st->cejs"
    real_mid = multiply(form_b, real_in, cos_b) - multiply(form_b, imag_in, sine_b)
    imag_mid = multiply(form_b, imag_in, cos_b) + multiply(form_b, real_in, sine_b)
    cos_t, sine_t = unit_table(
        count_up(outer_len)[:, None], count_up(inner_len)[None, :], block_len
    )
    real_mid, imag_mid = turn_backward(real_mid, imag_mid, cos_t, sine_t)
    cos_a, sine_a = unit_table(
        count_up(outer_len)[:, None], count_up(outer_len)[None, :], outer_len
    )
    form_a = "jk,cejs->ceks"
    real_out = multiply(form_a, cos_a, real_mid) - multiply(form_a, sine_a, imag_mid)
    imag_out = multiply(form_a, cos_a, imag_mid) + multiply(form_a, sine_a, real_mid)
    return (real_out.reshape(lead, pair, block_len), imag_out.reshape(lead, pair, block_len))


def local_columns(gate_proj, key_proj, value_proj, filter_taps, skip_gain):
    outer_count = lax.axis_size("outer")
    inner_count = lax.axis_size("inner")
    groups = outer_count * inner_count
    here = lax.axis_index(("outer", "inner"))
    chans, tok_local = gate_proj.shape
    half_chans = chans // 2
    span = tok_local // groups
    total_len = 2 * groups * tok_local
    signal = key_proj.astype(jnp.float32) * value_proj.astype(jnp.float32)
    taps_local = lax.all_gather(filter_taps, "chan", axis=0, tiled=True)
    sig_cols, tap_cols = (
        lax.all_to_all(
            signal.reshape(chans, groups, span),
            ("outer", "inner"),
            split_axis=1,
            concat_axis=1,
            tiled=True,
        ),
        lax.all_to_all(
            taps_local.reshape(1, groups, span),
            ("outer", "inner"),
            split_axis=1,
            concat_axis=1,
            tiled=True,
        ),
    )
    sig_real, sig_imag = column_forward_pair(
        sig_cols[:half_chans], sig_cols[half_chans:], groups, here, total_len
    )
    tap_real, tap_imag = column_forward(tap_cols, groups, here, total_len)
    sig_real, sig_imag, tap_real, tap_imag = (
        lax.all_to_all(sig_real, ("outer", "inner"), split_axis=1, concat_axis=2, tiled=True),
        lax.all_to_all(sig_imag, ("outer", "inner"), split_axis=1, concat_axis=2, tiled=True),
        lax.all_to_all(tap_real, ("outer", "inner"), split_axis=1, concat_axis=2, tiled=True),
        lax.all_to_all(tap_imag, ("outer", "inner"), split_axis=1, concat_axis=2, tiled=True),
    )
    sig_real, sig_imag = local_forward(sig_real, sig_imag)
    tap_real, tap_imag = local_forward(tap_real, tap_imag)
    prod_real = sig_real * tap_real - sig_imag * tap_imag
    prod_imag = sig_real * tap_imag + sig_imag * tap_real
    back_real, back_imag = local_backward(prod_real, prod_imag)
    back_real, back_imag = (
        lax.all_to_all(back_real, ("outer", "inner"), split_axis=2, concat_axis=1, tiled=True),
        lax.all_to_all(back_imag, ("outer", "inner"), split_axis=2, concat_axis=1, tiled=True),
    )
    positions = here * span + count_up(span)
    cos_r, sine_r = unit_table(count_up(2 * groups)[:, None], positions[None, :], total_len)
    back_real, back_imag = turn_backward(back_real, back_imag, cos_r, sine_r)
    cos_m, sine_m = unit_table(count_up(2 * groups)[:, None], count_up(groups)[None, :], 2 * groups)
    form_m = "am,car->cmr"
    conv_real = multiply(form_m, cos_m, back_real) - multiply(form_m, sine_m, back_imag)
    conv_imag = multiply(form_m, cos_m, back_imag) + multiply(form_m, sine_m, back_real)
    conv_cols = jnp.concatenate((conv_real, conv_imag), axis=0)
    conv_cols = conv_cols * (1.0 / total_len)
    conv = lax.all_to_all(
        conv_cols, ("outer", "inner"), split_axis=1, concat_axis=2, tiled=True
    ).reshape(chans, tok_local)
    return gate_proj.astype(jnp.float32) * (conv + skip_gain[:, None] * signal)


LANES = 128
COLS = 256
MESH = pl.DeviceIdType.MESH


def split_np(table):
    high = table.astype(jnp.bfloat16)
    low = (table - high.astype(np.float64)).astype(jnp.bfloat16)
    return np.stack((high, low))


@functools.lru_cache(maxsize=None)
def dft_tables(rows):
    freqs = 2 * rows
    total_len = freqs * COLS
    angle_a = np.outer(np.arange(freqs), np.arange(freqs)) % freqs * (2.0 * np.pi / freqs)
    cos_a, sine_a = np.cos(angle_a), np.sin(angle_a)
    angle_b = np.outer(np.arange(COLS), np.arange(COLS)) % COLS * (2.0 * np.pi / COLS)
    cos_b, sine_b = np.cos(angle_b), np.sin(angle_b)
    angle_t = np.outer(np.arange(freqs), np.arange(COLS)) * (2.0 * np.pi / total_len)
    return (
        split_np(np.concatenate((cos_a[:, :rows], sine_a[:, :rows]), axis=1)),
        split_np(np.concatenate((cos_a[:rows], sine_a[:rows]), axis=1)),
        split_np(np.block([[cos_b, -sine_b], [sine_b, cos_b]])),
        np.stack((np.cos(angle_t), np.sin(angle_t))).astype(np.float32),
    )


def split(value):
    high = value.astype(jnp.bfloat16)
    return high, (value - high.astype(jnp.float32)).astype(jnp.bfloat16)


def dot(left, right, dims=((1,), (0,))):
    return lax.dot_general(left, right, (dims, ((), ())), preferred_element_type=jnp.float32)


def dot3(left_hi, left_lo, right_hi, right_lo, dims=((1,), (0,))):
    return (
        dot(left_lo, right_hi, dims) + dot(left_hi, right_lo, dims) + dot(left_hi, right_hi, dims)
    )


def flip(index, bits):
    for k in range(bits.bit_length()):
        if bits >> k & 1:
            index = index + (1 - 2 * (index // 2**k % 2)) * 2**k
    return index


def conv_kernel(
    sizes,
    gate_hbm,
    key_hbm,
    value_hbm,
    tap_ref,
    skip_ref,
    fwd_hbm,
    inv_hbm,
    col_hbm,
    twid_hbm,
    out_ref,
    gate,
    key,
    value,
    sig,
    conv,
    xbuf,
    hbuf,
    ybuf,
    rhs,
    back,
    spec,
    fwd,
    inv,
    col,
    twid,
    sig_send,
    sig_recv,
    out_send,
    out_recv,
    tap_send,
    tap_recv,
    spread_send,
    spread_recv,
    own_sem,
    table_sem,
    load_sem,
):
    outer_n, inner_n, chan_n = sizes
    groups = outer_n * inner_n
    chans, tok_local = out_ref.shape
    tiles = tok_local // LANES
    mine_n = chans // groups
    pairs = mine_n // 2
    rows = groups * tiles // 2
    freqs = 2 * rows
    step = 256
    outer = lax.axis_index("outer")
    inner = lax.axis_index("inner")
    chan = lax.axis_index("chan")
    here = outer * inner_n + inner
    hops = [(dz, dx) for dz in range(outer_n)[::-1] for dx in range(inner_n)[::-1] if dz or dx]
    peers = []
    for dz, dx in hops:
        to_z, to_x = flip(outer, dz), flip(inner, dx)
        peers.append((to_z * inner_n + to_x, (to_z, to_x, chan)))
    sides = [(outer, inner, flip(chan, dc)) for dc in range(1, chan_n)]

    barrier = pltpu.get_barrier_semaphore()
    for _, where in peers:
        pl.semaphore_signal(barrier, inc=1, device_id=where, device_id_type=MESH)
    for where in sides:
        pl.semaphore_signal(barrier, inc=1, device_id=where, device_id_type=MESH)

    loads = [
        pltpu.make_async_copy(src, dst, load_sem.at[k])
        for k, (src, dst) in enumerate(((key_hbm, key), (value_hbm, value), (gate_hbm, gate)))
    ]
    for copy in loads:
        copy.start()
    loads[0].wait()
    loads[1].wait()

    def product_step(t, carry):
        lanes = pl.ds(pl.multiple_of(t * LANES, LANES), LANES)
        prod = key[:, lanes].astype(jnp.float32) * value[:, lanes].astype(jnp.float32)
        for k in range(chans // 8):
            sig[pl.ds(8 * k * tiles + t, 8, stride=tiles), :] = prod[8 * k : 8 * k + 8]
        return carry

    lax.fori_loop(0, tiles, product_step, 0, unroll=8)
    pl.semaphore_wait(barrier, len(peers) + len(sides))

    def remote(src, dst, send, recv, where):
        copy = pltpu.make_async_remote_copy(
            src_ref=src,
            dst_ref=dst,
            send_sem=send,
            recv_sem=recv,
            device_id=where,
            device_id_type=MESH,
        )
        copy.start()
        return copy

    def outside(ref, owner, which):
        first = pl.multiple_of((owner * mine_n + which) * tiles, 8)
        return ref.at[pl.ds(first, tiles)]

    def inside(ref, place, which):
        first = pl.multiple_of((which * groups + place) * tiles, 8)
        return ref.at[pl.ds(first, tiles)]

    tap_copies = [
        remote(tap_ref, hbuf.at[here, chan], tap_send.at[j], tap_recv.at[j], where)
        for j, (_, where) in enumerate(peers)
    ]
    own = [pltpu.make_async_copy(tap_ref, hbuf.at[here, chan], own_sem.at[2 * mine_n])]
    own[0].start()
    sig_copies = []
    for pair in range(pairs):
        sig_copies.append(
            [
                remote(
                    outside(sig, dest, which),
                    inside(xbuf, here, which),
                    sig_send.at[which, j],
                    sig_recv.at[which, j],
                    where,
                )
                for j, (dest, where) in enumerate(peers)
                for which in (2 * pair, 2 * pair + 1)
            ]
        )
    for which in range(mine_n):
        keep = pltpu.make_async_copy(
            outside(sig, here, which), inside(xbuf, here, which), own_sem.at[which]
        )
        keep.start()
        own.append(keep)
    tables = [
        pltpu.make_async_copy(src, dst, table_sem.at[i])
        for i, (src, dst) in enumerate(
            ((fwd_hbm, fwd), (col_hbm, col), (twid_hbm, twid), (inv_hbm, inv))
        )
    ]
    for copy in tables:
        copy.start()

    own[0].wait()
    for copy in tap_copies:
        copy.wait_recv()
    spread_copies = [
        remote(hbuf.at[:, chan], hbuf.at[:, chan], spread_send.at[j], spread_recv.at[j], where)
        for j, where in enumerate(sides)
    ]

    square = (chans, chans)
    diagonal = lax.broadcasted_iota(jnp.int32, square, 0) == lax.broadcasted_iota(jnp.int32, square, 1)
    skips = jnp.sum(
        jnp.where(diagonal, jnp.broadcast_to(skip_ref[...], square), 0.0), axis=1, keepdims=True
    )

    def direct_step(t, carry):
        lanes = pl.ds(pl.multiple_of(t * LANES, LANES), LANES)
        prod = key[:, lanes].astype(jnp.float32) * value[:, lanes].astype(jnp.float32)
        out_ref[:, lanes] = skips * prod
        return carry

    lax.fori_loop(0, tiles, direct_step, 0, unroll=4)
    for copy in tables:
        copy.wait()
    for copy in spread_copies:
        copy.wait_recv()

    def fill(real, imag):
        for half in range(2):
            for part, at, sign in (
                (real, (0, 0), 1.0),
                (imag, (0, 1), 1.0),
                (imag, (1, 0), 1.0),
                (real, (1, 1), -1.0),
            ):
                lanes = pl.ds(at[1] * COLS + half * LANES, LANES)
                if part is None:
                    high = low = jnp.zeros((rows, LANES), jnp.bfloat16)
                else:
                    high, low = split(sign * part(half))
                rhs[0, pl.ds(at[0] * rows, rows), lanes] = high
                rhs[1, pl.ds(at[0] * rows, rows), lanes] = low

    def forward(at):
        mid = dot3(fwd[0, at, :], fwd[1, at, :], rhs[0], rhs[1])
        real, imag = mid[:, :COLS], mid[:, COLS:]
        cos_t, sine_t = twid[0, at, :], twid[1, at, :]
        turned = jnp.concatenate(turn_forward(real, imag, cos_t, sine_t), axis=1)
        return dot3(*split(turned), col[0], col[1])

    tap_rows = hbuf.shape[2]
    fill(
        lambda half: hbuf[:, :, pl.ds(half, tap_rows // 2, stride=2), :].reshape(rows, LANES), None
    )

    def filter_step(t, carry):
        at = pl.ds(pl.multiple_of(t * step, step), step)
        spec[at, :] = forward(at) * (1.0 / (freqs * COLS))
        return carry

    lax.fori_loop(0, freqs // step, filter_step, 0)

    out_copies = []
    for pair in range(pairs):
        own[1 + 2 * pair].wait()
        own[2 + 2 * pair].wait()
        for copy in sig_copies[pair]:
            copy.wait_recv()

        def part(which):
            return lambda half: xbuf[pl.ds(which * freqs + half, rows, stride=2), :]

        fill(part(2 * pair), part(2 * pair + 1))

        def pair_step(t, carry):
            at = pl.ds(pl.multiple_of(t * step, step), step)
            below = pl.ds(pl.multiple_of(t * step + freqs, step), step)
            freq = forward(at)
            real, imag = freq[:, :COLS], freq[:, COLS:]
            spec_real, spec_imag = spec[at, :COLS], spec[at, COLS:]
            prod = jnp.concatenate(
                (real * spec_real - imag * spec_imag, real * spec_imag + imag * spec_real), axis=1
            )
            mid = dot3(*split(prod), col[0], col[1], ((1,), (1,)))
            cos_t, sine_t = twid[0, at, :], twid[1, at, :]
            real, imag = turn_backward(mid[:, :COLS], mid[:, COLS:], cos_t, sine_t)
            real_hi, real_lo = split(real)
            imag_hi, imag_lo = split(imag)
            back[0, at, :COLS] = real_hi
            back[1, at, :COLS] = real_lo
            back[0, at, COLS:] = imag_hi
            back[1, at, COLS:] = imag_lo
            back[0, below, :COLS] = -imag_hi
            back[1, below, :COLS] = -imag_lo
            back[0, below, COLS:] = real_hi
            back[1, below, COLS:] = real_lo
            return carry

        lax.fori_loop(0, freqs // step, pair_step, 0)
        result = dot3(inv[0], inv[1], back[0], back[1])
        for which in range(2):
            for half in range(2):
                first = which * COLS + half * LANES
                place = pl.ds((2 * pair + which) * freqs + half, rows, stride=2)
                ybuf[place, :] = result[:, first : first + LANES]
        out_copies.append(
            [
                remote(
                    inside(ybuf, dest, which),
                    outside(conv, here, which),
                    out_send.at[which, j],
                    out_recv.at[which, j],
                    where,
                )
                for j, (dest, where) in enumerate(peers)
                for which in (2 * pair, 2 * pair + 1)
            ]
        )
        for which in (2 * pair, 2 * pair + 1):
            keep = pltpu.make_async_copy(
                inside(ybuf, here, which), outside(conv, here, which), own_sem.at[mine_n + which]
            )
            keep.start()
            own.append(keep)

    loads[2].wait()
    for copy in own[1 + mine_n :]:
        copy.wait()
    for copy in sum(out_copies, []):
        copy.wait_recv()

    def gate_step(t, carry):
        lanes = pl.ds(pl.multiple_of(t * LANES, LANES), LANES)
        gates = gate[:, lanes].astype(jnp.float32)
        for k in range(chans // 8):
            at = pl.ds(8 * k, 8)
            mixed = conv[pl.ds(8 * k * tiles + t, 8, stride=tiles), :] + out_ref[at, lanes]
            out_ref[at, lanes] = gates[8 * k : 8 * k + 8] * mixed
        return carry

    lax.fori_loop(0, tiles, gate_step, 0, unroll=8)
    for copy in tap_copies + spread_copies + sum(sig_copies, []) + sum(out_copies, []):
        copy.wait_send()


def keep_hbm(array):
    return pltpu.with_memory_space_constraint(array, pltpu.HBM)


def local_whole(gate_proj, key_proj, value_proj, filter_taps, skip_gain):
    sizes = tuple(lax.axis_size(name) for name in ("outer", "inner", "chan"))
    groups = sizes[0] * sizes[1]
    chans, tok_local = gate_proj.shape
    mine_n = chans // groups
    rows = groups * tok_local // COLS
    tap_rows = filter_taps.shape[0] // LANES
    dma = pltpu.SemaphoreType.DMA
    vmem = pl.BlockSpec(memory_space=pltpu.VMEM)
    hbm = pl.BlockSpec(memory_space=pltpu.HBM)
    tables = dft_tables(rows)
    return pl.pallas_call(
        functools.partial(conv_kernel, sizes),
        out_shape=jax.ShapeDtypeStruct((chans, tok_local), jnp.float32),
        in_specs=[hbm, hbm, hbm, vmem, vmem, hbm, hbm, hbm, hbm],
        out_specs=vmem,
        scratch_shapes=[
            pltpu.VMEM((chans, tok_local), gate_proj.dtype),
            pltpu.VMEM((chans, tok_local), key_proj.dtype),
            pltpu.VMEM((chans, tok_local), value_proj.dtype),
            pltpu.VMEM((chans * tok_local // LANES, LANES), jnp.float32),
            pltpu.VMEM((chans * tok_local // LANES, LANES), jnp.float32),
            pltpu.VMEM((mine_n * 2 * rows, LANES), jnp.float32),
            pltpu.VMEM((groups, sizes[2], tap_rows, LANES), jnp.float32),
            pltpu.VMEM((mine_n * 2 * rows, LANES), jnp.float32),
            pltpu.VMEM((2, 2 * rows, 2 * COLS), jnp.bfloat16),
            pltpu.VMEM((2, 4 * rows, 2 * COLS), jnp.bfloat16),
            pltpu.VMEM((2 * rows, 2 * COLS), jnp.float32),
            pltpu.VMEM(tables[0].shape, jnp.bfloat16),
            pltpu.VMEM(tables[1].shape, jnp.bfloat16),
            pltpu.VMEM(tables[2].shape, jnp.bfloat16),
            pltpu.VMEM(tables[3].shape, jnp.float32),
            dma((mine_n, groups - 1)),
            dma((mine_n, groups - 1)),
            dma((mine_n, groups - 1)),
            dma((mine_n, groups - 1)),
            dma((groups - 1,)),
            dma((groups - 1,)),
            dma((sizes[2] - 1,)),
            dma((sizes[2] - 1,)),
            dma((2 * mine_n + 1,)),
            dma((4,)),
            dma((3,)),
        ],
        compiler_params=pltpu.CompilerParams(
            collective_id=0, has_side_effects=True, vmem_limit_bytes=48 * 1024 * 1024
        ),
    )(
        keep_hbm(gate_proj),
        keep_hbm(key_proj),
        keep_hbm(value_proj),
        keep_hbm(filter_taps.reshape(tap_rows, LANES)),
        keep_hbm(skip_gain[None, :]),
        *(keep_hbm(jnp.asarray(table)) for table in tables),
    )


def power_of_two(number):
    return number & (number - 1) == 0


def local(gate_proj, key_proj, value_proj, filter_taps, skip_gain):
    groups = lax.axis_size("outer") * lax.axis_size("inner")
    whole_pairs = gate_proj.shape[0] % (2 * groups) == 0
    flips = all(power_of_two(lax.axis_size(name)) for name in ("outer", "inner", "chan"))
    tiled = flips and gate_proj.shape[1] % (8 * COLS) == 0 and filter_taps.shape[0] % (8 * COLS) == 0
    one = local_whole if whole_pairs and tiled else local_columns
    return one(gate_proj, key_proj, value_proj, filter_taps, skip_gain)


def solution(mesh):
    placed = (
        P("chan", ("outer", "inner")),
        P("chan", ("outer", "inner")),
        P("chan", ("outer", "inner")),
        P(("outer", "inner", "chan")),
        P("chan"),
    )
    return jax.shard_map(
        local, mesh=mesh, in_specs=placed, out_specs=P("chan", ("outer", "inner")), check_vma=False
    )
```

```python
import functools
import math

import jax
import jax.numpy as jnp
import numpy as np
from jax import lax
from jax.experimental import pallas as pl
from jax.experimental.pallas import tpu as pltpu
from jax.sharding import PartitionSpec as P

HIGHEST = lax.Precision.HIGHEST


def count_up(length):
    return jnp.arange(length, dtype=jnp.int32)


def unit_table(row_index, col_index, modulus):
    turns = row_index * col_index % modulus
    angles = turns.astype(jnp.float32) * (2.0 * math.pi / modulus)
    return (jnp.cos(angles), jnp.sin(angles))


def multiply(form, left, right):
    return jnp.einsum(form, left, right, precision=HIGHEST)


def turn_forward(real_in, imag_in, cos_tab, sine_tab):
    return (real_in * cos_tab + imag_in * sine_tab, imag_in * cos_tab - real_in * sine_tab)


def turn_backward(real_in, imag_in, cos_tab, sine_tab):
    return (real_in * cos_tab - imag_in * sine_tab, imag_in * cos_tab + real_in * sine_tab)


def column_forward(columns, groups, here, total_len):
    span = columns.shape[2]
    cos_m, sine_m = unit_table(count_up(2 * groups)[:, None], count_up(groups)[None, :], 2 * groups)
    real_col = multiply("am,cmr->car", cos_m, columns)
    imag_col = -multiply("am,cmr->car", sine_m, columns)
    positions = here * span + count_up(span)
    cos_r, sine_r = unit_table(count_up(2 * groups)[:, None], positions[None, :], total_len)
    return turn_forward(real_col, imag_col, cos_r, sine_r)


def column_forward_pair(real_cols, imag_cols, groups, here, total_len):
    span = real_cols.shape[2]
    cos_m, sine_m = unit_table(count_up(2 * groups)[:, None], count_up(groups)[None, :], 2 * groups)
    form = "am,cmr->car"
    real_col = multiply(form, cos_m, real_cols) + multiply(form, sine_m, imag_cols)
    imag_col = multiply(form, cos_m, imag_cols) - multiply(form, sine_m, real_cols)
    positions = here * span + count_up(span)
    cos_r, sine_r = unit_table(count_up(2 * groups)[:, None], positions[None, :], total_len)
    return turn_forward(real_col, imag_col, cos_r, sine_r)


def local_forward(real_in, imag_in):
    lead, pair, block_len = real_in.shape
    inner_len = 128
    outer_len = block_len // inner_len
    real_in = real_in.reshape(lead, pair, outer_len, inner_len)
    imag_in = imag_in.reshape(lead, pair, outer_len, inner_len)
    cos_a, sine_a = unit_table(
        count_up(outer_len)[:, None], count_up(outer_len)[None, :], outer_len
    )
    form_a = "jk,ceks->cejs"
    real_mid = multiply(form_a, cos_a, real_in) + multiply(form_a, sine_a, imag_in)
    imag_mid = multiply(form_a, cos_a, imag_in) - multiply(form_a, sine_a, real_in)
    cos_t, sine_t = unit_table(
        count_up(outer_len)[:, None], count_up(inner_len)[None, :], block_len
    )
    real_mid, imag_mid = turn_forward(real_mid, imag_mid, cos_t, sine_t)
    cos_b, sine_b = unit_table(
        count_up(inner_len)[:, None], count_up(inner_len)[None, :], inner_len
    )
    form_b = "cejs,st->cejt"
    real_out = multiply(form_b, real_mid, cos_b) + multiply(form_b, imag_mid, sine_b)
    imag_out = multiply(form_b, imag_mid, cos_b) - multiply(form_b, real_mid, sine_b)
    return (real_out, imag_out)


def local_backward(real_in, imag_in):
    lead, pair, outer_len, inner_len = real_in.shape
    block_len = outer_len * inner_len
    cos_b, sine_b = unit_table(
        count_up(inner_len)[:, None], count_up(inner_len)[None, :], inner_len
    )
    form_b = "cejt,st->cejs"
    real_mid = multiply(form_b, real_in, cos_b) - multiply(form_b, imag_in, sine_b)
    imag_mid = multiply(form_b, imag_in, cos_b) + multiply(form_b, real_in, sine_b)
    cos_t, sine_t = unit_table(
        count_up(outer_len)[:, None], count_up(inner_len)[None, :], block_len
    )
    real_mid, imag_mid = turn_backward(real_mid, imag_mid, cos_t, sine_t)
    cos_a, sine_a = unit_table(
        count_up(outer_len)[:, None], count_up(outer_len)[None, :], outer_len
    )
    form_a = "jk,cejs->ceks"
    real_out = multiply(form_a, cos_a, real_mid) - multiply(form_a, sine_a, imag_mid)
    imag_out = multiply(form_a, cos_a, imag_mid) + multiply(form_a, sine_a, real_mid)
    return (real_out.reshape(lead, pair, block_len), imag_out.reshape(lead, pair, block_len))


def local_columns(gate_proj, key_proj, value_proj, filter_taps, skip_gain):
    outer_count = lax.axis_size("outer")
    inner_count = lax.axis_size("inner")
    groups = outer_count * inner_count
    here = lax.axis_index(("outer", "inner"))
    chans, tok_local = gate_proj.shape
    half_chans = chans // 2
    span = tok_local // groups
    total_len = 2 * groups * tok_local
    signal = key_proj.astype(jnp.float32) * value_proj.astype(jnp.float32)
    taps_local = lax.all_gather(filter_taps, "chan", axis=0, tiled=True)
    sig_cols, tap_cols = (
        lax.all_to_all(
            signal.reshape(chans, groups, span),
            ("outer", "inner"),
            split_axis=1,
            concat_axis=1,
            tiled=True,
        ),
        lax.all_to_all(
            taps_local.reshape(1, groups, span),
            ("outer", "inner"),
            split_axis=1,
            concat_axis=1,
            tiled=True,
        ),
    )
    sig_real, sig_imag = column_forward_pair(
        sig_cols[:half_chans], sig_cols[half_chans:], groups, here, total_len
    )
    tap_real, tap_imag = column_forward(tap_cols, groups, here, total_len)
    sig_real, sig_imag, tap_real, tap_imag = (
        lax.all_to_all(sig_real, ("outer", "inner"), split_axis=1, concat_axis=2, tiled=True),
        lax.all_to_all(sig_imag, ("outer", "inner"), split_axis=1, concat_axis=2, tiled=True),
        lax.all_to_all(tap_real, ("outer", "inner"), split_axis=1, concat_axis=2, tiled=True),
        lax.all_to_all(tap_imag, ("outer", "inner"), split_axis=1, concat_axis=2, tiled=True),
    )
    sig_real, sig_imag = local_forward(sig_real, sig_imag)
    tap_real, tap_imag = local_forward(tap_real, tap_imag)
    prod_real = sig_real * tap_real - sig_imag * tap_imag
    prod_imag = sig_real * tap_imag + sig_imag * tap_real
    back_real, back_imag = local_backward(prod_real, prod_imag)
    back_real, back_imag = (
        lax.all_to_all(back_real, ("outer", "inner"), split_axis=2, concat_axis=1, tiled=True),
        lax.all_to_all(back_imag, ("outer", "inner"), split_axis=2, concat_axis=1, tiled=True),
    )
    positions = here * span + count_up(span)
    cos_r, sine_r = unit_table(count_up(2 * groups)[:, None], positions[None, :], total_len)
    back_real, back_imag = turn_backward(back_real, back_imag, cos_r, sine_r)
    cos_m, sine_m = unit_table(count_up(2 * groups)[:, None], count_up(groups)[None, :], 2 * groups)
    form_m = "am,car->cmr"
    conv_real = multiply(form_m, cos_m, back_real) - multiply(form_m, sine_m, back_imag)
    conv_imag = multiply(form_m, cos_m, back_imag) + multiply(form_m, sine_m, back_real)
    conv_cols = jnp.concatenate((conv_real, conv_imag), axis=0)
    conv_cols = conv_cols * (1.0 / total_len)
    conv = lax.all_to_all(
        conv_cols, ("outer", "inner"), split_axis=1, concat_axis=2, tiled=True
    ).reshape(chans, tok_local)
    return gate_proj.astype(jnp.float32) * (conv + skip_gain[:, None] * signal)


LANES = 128
COLS = 256
MESH = pl.DeviceIdType.MESH


def split_np(table):
    high = table.astype(jnp.bfloat16)
    low = (table - high.astype(np.float64)).astype(jnp.bfloat16)
    return np.stack((high, low))


@functools.lru_cache(maxsize=None)
def dft_tables(rows):
    freqs = 2 * rows
    total_len = freqs * COLS
    angle_a = np.outer(np.arange(freqs), np.arange(freqs)) % freqs * (2.0 * np.pi / freqs)
    cos_a, sine_a = np.cos(angle_a), np.sin(angle_a)
    angle_b = np.outer(np.arange(COLS), np.arange(COLS)) % COLS * (2.0 * np.pi / COLS)
    cos_b, sine_b = np.cos(angle_b), np.sin(angle_b)
    angle_t = np.outer(np.arange(freqs), np.arange(COLS)) * (2.0 * np.pi / total_len)
    return (
        split_np(np.concatenate((cos_a[:, :rows], sine_a[:, :rows]), axis=1)),
        split_np(np.concatenate((cos_a[:rows], sine_a[:rows]), axis=1)),
        split_np(np.block([[cos_b, -sine_b], [sine_b, cos_b]])),
        np.stack((np.cos(angle_t), np.sin(angle_t))).astype(np.float32),
    )


def split(value):
    high = value.astype(jnp.bfloat16)
    return high, (value - high.astype(jnp.float32)).astype(jnp.bfloat16)


def dot(left, right, dims=((1,), (0,))):
    return lax.dot_general(left, right, (dims, ((), ())), preferred_element_type=jnp.float32)


def dot3(left_hi, left_lo, right_hi, right_lo, dims=((1,), (0,))):
    return (
        dot(left_lo, right_hi, dims) + dot(left_hi, right_lo, dims) + dot(left_hi, right_hi, dims)
    )


def flip(index, bits):
    for k in range(bits.bit_length()):
        if bits >> k & 1:
            index = index + (1 - 2 * (index // 2**k % 2)) * 2**k
    return index


def conv_kernel(
    sizes,
    gate_hbm,
    key_hbm,
    value_hbm,
    tap_ref,
    skip_ref,
    fwd_hbm,
    inv_hbm,
    col_hbm,
    twid_hbm,
    out_ref,
    gate,
    key,
    value,
    sig,
    conv,
    xbuf,
    hbuf,
    ybuf,
    rhs,
    back,
    spec,
    fwd,
    inv,
    col,
    twid,
    sig_send,
    sig_recv,
    out_send,
    out_recv,
    tap_send,
    tap_recv,
    spread_send,
    spread_recv,
    own_sem,
    table_sem,
    load_sem,
    skip_buf,
):
    outer_n, inner_n, chan_n = sizes
    groups = outer_n * inner_n
    chans, tok_local = out_ref.shape
    tiles = tok_local // LANES
    mine_n = chans // groups
    plane = inner_n * mine_n
    pairs = mine_n // 2
    rows = groups * tiles // 2
    freqs = 2 * rows
    step = 256
    outer = lax.axis_index("outer")
    inner = lax.axis_index("inner")
    chan = lax.axis_index("chan")
    here = outer * inner_n + inner
    order = range(outer_n)[::-1]
    firsts = [pl.multiple_of(flip(outer, dz) * plane, 8) for dz in order]
    hops = [(dz, dx) for dz in order for dx in range(inner_n)[::-1] if dz or dx]
    peers = []
    for dz, dx in hops:
        to_z, to_x = flip(outer, dz), flip(inner, dx)
        peers.append((to_z * inner_n + to_x, (to_z, to_x, chan)))
    sides = [(outer, inner, flip(chan, dc)) for dc in range(1, chan_n)]

    barrier = pltpu.get_barrier_semaphore()
    for _, where in peers:
        pl.semaphore_signal(barrier, inc=1, device_id=where, device_id_type=MESH)
    for where in sides:
        pl.semaphore_signal(barrier, inc=1, device_id=where, device_id_type=MESH)

    loads = [
        pltpu.make_async_copy(src.at[pl.ds(firsts[i], plane)], dst.at[i], load_sem.at[i, k])
        for i in range(outer_n)
        for k, (src, dst) in enumerate(((key_hbm, key), (value_hbm, value)))
    ]
    for copy in loads:
        copy.start()

    def product(i, lanes):
        return key[i, :, lanes].astype(jnp.float32) * value[i, :, lanes].astype(jnp.float32)

    def make_signal(i):
        loads[2 * i].wait()
        loads[2 * i + 1].wait()

        def product_step(t, carry):
            prod = product(i, pl.ds(pl.multiple_of(t * LANES, LANES), LANES))
            for k in range(plane // 8):
                start = (firsts[i] + 8 * k) * tiles + t
                sig[pl.ds(start, 8, stride=tiles), :] = prod[8 * k : 8 * k + 8]
            return carry

        lax.fori_loop(0, tiles, product_step, 0, unroll=8)

    make_signal(0)
    pl.semaphore_wait(barrier, len(peers) + len(sides))

    def remote(src, dst, send, recv, where):
        copy = pltpu.make_async_remote_copy(
            src_ref=src,
            dst_ref=dst,
            send_sem=send,
            recv_sem=recv,
            device_id=where,
            device_id_type=MESH,
        )
        copy.start()
        return copy

    def outside(ref, owner, which):
        first = pl.multiple_of((owner * mine_n + which) * tiles, 8)
        return ref.at[pl.ds(first, tiles)]

    def inside(ref, place, which):
        first = pl.multiple_of((which * groups + place) * tiles, 8)
        return ref.at[pl.ds(first, tiles)]

    tap_copies = [
        remote(tap_ref, hbuf.at[here, chan], tap_send.at[j], tap_recv.at[j], where)
        for j, (_, where) in enumerate(peers)
    ]
    own = [pltpu.make_async_copy(tap_ref, hbuf.at[here, chan], own_sem.at[2 * mine_n])]
    own[0].start()
    sig_copies = [[] for _ in range(pairs)]

    def send_signal(i, pair):
        for j, (dest, where) in enumerate(peers):
            if hops[j][0] == order[i]:
                for which in (2 * pair, 2 * pair + 1):
                    sig_copies[pair].append(
                        remote(
                            outside(sig, dest, which),
                            inside(xbuf, here, which),
                            sig_send.at[which, j],
                            sig_recv.at[which, j],
                            where,
                        )
                    )

    for i in range(outer_n):
        if i:
            make_signal(i)
        send_signal(i, 0)
    for pair in range(1, pairs):
        for i in range(outer_n):
            send_signal(i, pair)
    for which in range(mine_n):
        keep = pltpu.make_async_copy(
            outside(sig, here, which), inside(xbuf, here, which), own_sem.at[which]
        )
        keep.start()
        own.append(keep)
    tables = [
        pltpu.make_async_copy(src, dst, table_sem.at[i])
        for i, (src, dst) in enumerate(
            ((fwd_hbm, fwd), (col_hbm, col), (twid_hbm, twid), (inv_hbm, inv))
        )
    ]
    gates = [
        pltpu.make_async_copy(
            gate_hbm.at[pl.ds(firsts[i], plane)], gate.at[i], load_sem.at[i, 2]
        )
        for i in range(outer_n)
    ]
    for copy in tables + gates:
        copy.start()

    own[0].wait()
    for copy in tap_copies:
        copy.wait_recv()
    spread_copies = [
        remote(hbuf.at[:, chan], hbuf.at[:, chan], spread_send.at[j], spread_recv.at[j], where)
        for j, where in enumerate(sides)
    ]

    square = (chans, chans)
    diagonal = lax.broadcasted_iota(jnp.int32, square, 0) == lax.broadcasted_iota(jnp.int32, square, 1)
    skips = jnp.sum(
        jnp.where(diagonal, jnp.broadcast_to(skip_ref[...], square), 0.0), axis=1, keepdims=True
    )

    skip_buf[...] = jnp.broadcast_to(skips, (chans, LANES))

    def direct_step(t, carry):
        lanes = pl.ds(pl.multiple_of(t * LANES, LANES), LANES)
        for i in range(outer_n):
            at = pl.ds(firsts[i], plane)
            out_ref[at, lanes] = skip_buf[at, :] * product(i, lanes)
        return carry

    lax.fori_loop(0, tiles, direct_step, 0, unroll=4)
    for copy in tables:
        copy.wait()
    for copy in spread_copies:
        copy.wait_recv()

    def fill(real, imag):
        for half in range(2):
            for part, at, sign in (
                (real, (0, 0), 1.0),
                (imag, (0, 1), 1.0),
                (imag, (1, 0), 1.0),
                (real, (1, 1), -1.0),
            ):
                lanes = pl.ds(at[1] * COLS + half * LANES, LANES)
                if part is None:
                    high = low = jnp.zeros((rows, LANES), jnp.bfloat16)
                else:
                    high, low = split(sign * part(half))
                rhs[0, pl.ds(at[0] * rows, rows), lanes] = high
                rhs[1, pl.ds(at[0] * rows, rows), lanes] = low

    def forward(at):
        mid = dot3(fwd[0, at, :], fwd[1, at, :], rhs[0], rhs[1])
        real, imag = mid[:, :COLS], mid[:, COLS:]
        cos_t, sine_t = twid[0, at, :], twid[1, at, :]
        turned = jnp.concatenate(turn_forward(real, imag, cos_t, sine_t), axis=1)
        return dot3(*split(turned), col[0], col[1])

    tap_rows = hbuf.shape[2]
    fill(
        lambda half: hbuf[:, :, pl.ds(half, tap_rows // 2, stride=2), :].reshape(rows, LANES), None
    )

    def filter_step(t, carry):
        at = pl.ds(pl.multiple_of(t * step, step), step)
        spec[at, :] = forward(at) * (1.0 / (freqs * COLS))
        return carry

    lax.fori_loop(0, freqs // step, filter_step, 0)

    out_copies = []
    for pair in range(pairs):
        own[1 + 2 * pair].wait()
        own[2 + 2 * pair].wait()
        for copy in sig_copies[pair]:
            copy.wait_recv()

        def part(which):
            return lambda half: xbuf[pl.ds(which * freqs + half, rows, stride=2), :]

        fill(part(2 * pair), part(2 * pair + 1))

        def pair_step(t, carry):
            at = pl.ds(pl.multiple_of(t * step, step), step)
            below = pl.ds(pl.multiple_of(t * step + freqs, step), step)
            freq = forward(at)
            real, imag = freq[:, :COLS], freq[:, COLS:]
            spec_real, spec_imag = spec[at, :COLS], spec[at, COLS:]
            prod = jnp.concatenate(
                (real * spec_real - imag * spec_imag, real * spec_imag + imag * spec_real), axis=1
            )
            mid = dot3(*split(prod), col[0], col[1], ((1,), (1,)))
            cos_t, sine_t = twid[0, at, :], twid[1, at, :]
            real, imag = turn_backward(mid[:, :COLS], mid[:, COLS:], cos_t, sine_t)
            real_hi, real_lo = split(real)
            imag_hi, imag_lo = split(imag)
            back[0, at, :COLS] = real_hi
            back[1, at, :COLS] = real_lo
            back[0, at, COLS:] = imag_hi
            back[1, at, COLS:] = imag_lo
            back[0, below, :COLS] = -imag_hi
            back[1, below, :COLS] = -imag_lo
            back[0, below, COLS:] = real_hi
            back[1, below, COLS:] = real_lo
            return carry

        lax.fori_loop(0, freqs // step, pair_step, 0)
        result = dot3(inv[0], inv[1], back[0], back[1])
        for which in range(2):
            for half in range(2):
                first = which * COLS + half * LANES
                place = pl.ds((2 * pair + which) * freqs + half, rows, stride=2)
                ybuf[place, :] = result[:, first : first + LANES]
        out_copies.append(
            [
                remote(
                    inside(ybuf, dest, which),
                    outside(conv, here, which),
                    out_send.at[which, j],
                    out_recv.at[which, j],
                    where,
                )
                for j, (dest, where) in enumerate(peers)
                for which in (2 * pair, 2 * pair + 1)
            ]
        )
        for which in (2 * pair, 2 * pair + 1):
            keep = pltpu.make_async_copy(
                inside(ybuf, here, which), outside(conv, here, which), own_sem.at[mine_n + which]
            )
            keep.start()
            own.append(keep)

    def gate_plane(i):
        def gate_step(t, carry):
            lanes = pl.ds(pl.multiple_of(t * LANES, LANES), LANES)
            factor = gate[i, :, lanes].astype(jnp.float32)
            for k in range(plane // 8):
                at = pl.ds(pl.multiple_of(firsts[i] + 8 * k, 8), 8)
                start = (firsts[i] + 8 * k) * tiles + t
                mixed = conv[pl.ds(start, 8, stride=tiles), :] + out_ref[at, lanes]
                out_ref[at, lanes] = factor[8 * k : 8 * k + 8] * mixed
            return carry

        lax.fori_loop(0, tiles, gate_step, 0, unroll=8)

    for i in reversed(range(outer_n)):
        gates[i].wait()
        if order[i] == 0:
            for copy in own[1 + mine_n :]:
                copy.wait()
        for pair in range(pairs):
            for n, copy in enumerate(out_copies[pair]):
                if hops[n // 2][0] == order[i]:
                    copy.wait_recv()
        gate_plane(i)
    for copy in tap_copies + spread_copies + sum(sig_copies, []) + sum(out_copies, []):
        copy.wait_send()


def keep_hbm(array):
    return pltpu.with_memory_space_constraint(array, pltpu.HBM)


def local_whole(gate_proj, key_proj, value_proj, filter_taps, skip_gain):
    sizes = tuple(lax.axis_size(name) for name in ("outer", "inner", "chan"))
    groups = sizes[0] * sizes[1]
    chans, tok_local = gate_proj.shape
    mine_n = chans // groups
    rows = groups * tok_local // COLS
    tap_rows = filter_taps.shape[0] // LANES
    dma = pltpu.SemaphoreType.DMA
    vmem = pl.BlockSpec(memory_space=pltpu.VMEM)
    hbm = pl.BlockSpec(memory_space=pltpu.HBM)
    tables = dft_tables(rows)
    return pl.pallas_call(
        functools.partial(conv_kernel, sizes),
        out_shape=jax.ShapeDtypeStruct((chans, tok_local), jnp.float32),
        in_specs=[hbm, hbm, hbm, vmem, vmem, hbm, hbm, hbm, hbm],
        out_specs=vmem,
        scratch_shapes=[
            pltpu.VMEM((sizes[0], chans // sizes[0], tok_local), gate_proj.dtype),
            pltpu.VMEM((sizes[0], chans // sizes[0], tok_local), key_proj.dtype),
            pltpu.VMEM((sizes[0], chans // sizes[0], tok_local), value_proj.dtype),
            pltpu.VMEM((chans * tok_local // LANES, LANES), jnp.float32),
            pltpu.VMEM((chans * tok_local // LANES, LANES), jnp.float32),
            pltpu.VMEM((mine_n * 2 * rows, LANES), jnp.float32),
            pltpu.VMEM((groups, sizes[2], tap_rows, LANES), jnp.float32),
            pltpu.VMEM((mine_n * 2 * rows, LANES), jnp.float32),
            pltpu.VMEM((2, 2 * rows, 2 * COLS), jnp.bfloat16),
            pltpu.VMEM((2, 4 * rows, 2 * COLS), jnp.bfloat16),
            pltpu.VMEM((2 * rows, 2 * COLS), jnp.float32),
            pltpu.VMEM(tables[0].shape, jnp.bfloat16),
            pltpu.VMEM(tables[1].shape, jnp.bfloat16),
            pltpu.VMEM(tables[2].shape, jnp.bfloat16),
            pltpu.VMEM(tables[3].shape, jnp.float32),
            dma((mine_n, groups - 1)),
            dma((mine_n, groups - 1)),
            dma((mine_n, groups - 1)),
            dma((mine_n, groups - 1)),
            dma((groups - 1,)),
            dma((groups - 1,)),
            dma((sizes[2] - 1,)),
            dma((sizes[2] - 1,)),
            dma((2 * mine_n + 1,)),
            dma((4,)),
            dma((sizes[0], 3)),
            pltpu.VMEM((chans, LANES), jnp.float32),
        ],
        compiler_params=pltpu.CompilerParams(
            collective_id=0, has_side_effects=True, vmem_limit_bytes=48 * 1024 * 1024
        ),
    )(
        keep_hbm(gate_proj),
        keep_hbm(key_proj),
        keep_hbm(value_proj),
        keep_hbm(filter_taps.reshape(tap_rows, LANES)),
        keep_hbm(skip_gain[None, :]),
        *(keep_hbm(jnp.asarray(table)) for table in tables),
    )


def power_of_two(number):
    return number & (number - 1) == 0


def local(gate_proj, key_proj, value_proj, filter_taps, skip_gain):
    groups = lax.axis_size("outer") * lax.axis_size("inner")
    whole_pairs = gate_proj.shape[0] % (2 * groups) == 0
    flips = all(power_of_two(lax.axis_size(name)) for name in ("outer", "inner", "chan"))
    tiled = flips and gate_proj.shape[1] % (8 * COLS) == 0 and filter_taps.shape[0] % (8 * COLS) == 0
    tiled = tiled and gate_proj.shape[0] // lax.axis_size("outer") % 8 == 0
    one = local_whole if whole_pairs and tiled else local_columns
    return one(gate_proj, key_proj, value_proj, filter_taps, skip_gain)


def solution(mesh):
    placed = (
        P("chan", ("outer", "inner")),
        P("chan", ("outer", "inner")),
        P("chan", ("outer", "inner")),
        P(("outer", "inner", "chan")),
        P("chan"),
    )
    return jax.shard_map(
        local, mesh=mesh, in_specs=placed, out_specs=P("chan", ("outer", "inner")), check_vma=False
    )
```
